32 devices in a mesh: expert: 2 (over x), dp: 16 (over z, y, core).
Axes of the slice: x: 2, y: 2, z: 4, core: 2. Of those that a mesh axis runs over, the one named last changes fastest.
Arguments:
- tokens: bfloat16 [4096, 3072], P(('expert', 'dp')), may hold values from -6 to 6
- out_grad: bfloat16 [4096, 3072], P(('expert', 'dp')), may hold values from -6 to 6
- routes: int32 [4096, 2], P(('expert', 'dp')), may hold values from 0 to 7, all different within a row; in each aligned block of 128 rows (0 to 127, 128 to 255, ...) at most 40 rows name the same one
- gates: float32 [4096, 2], P(('expert', 'dp')), may hold values from 0.2 to 1
- w_gate: bfloat16 [8, 3072, 128], P('expert', 'dp'), may hold values from -0.109375 to 0.109375
- w_up: bfloat16 [8, 3072, 128], P('expert', 'dp'), may hold values from -0.109375 to 0.109375
- w_down_t: bfloat16 [8, 3072, 128], P('expert', 'dp'), may hold values from -0.5 to 0.5
Outputs:
- token_grad: bfloat16 [4096, 3072], P(('expert', 'dp'))
- grad_gate: float32 [8, 3072, 128], P('expert', 'dp')
- grad_up: float32 [8, 3072, 128], P('expert', 'dp')
The draws below stay inside these ranges and needn't reach their ends.
Inputs may be any that keep to these rules, and one draw needn't show every extreme that they name: `routes`: each row names two different experts. No expert is named by more than 40 of the rows of one device, and in every draw some device names some expert exactly 40 times.
All inputs are finite; a program needn't handle non-finite values.
Results may differ from the reference program's by a relative error of at most 0.0065.
Values may be sent and summed in bfloat16 or wider, within the bound.
A program may use at most 64 MiB of HBM per device.

```python
import math
import jax
import jax.numpy as jnp
import numpy as np
from jax import lax

D = 3072
FF = 128
EXPERTS = 8
TOK_DEV = 128
CAP = 40
TOKENS = 4096
DEVICES = 32


def spiked(array, own_key, source, target, blocks, factor):
    owner, partner = [(jnp.arange(array.shape[position]) // (array.shape[position] // blocks)).reshape([-1 if axis == position else 1 for axis in range(array.ndim)]) for position in (source, target)]
    chosen = jax.random.permutation(own_key, blocks)[partner]
    strong = (owner == chosen) | (owner == (partner + blocks // 2) % blocks)
    return jnp.where(strong, factor * array, array)


def block_scale(key, extent, cuts, least, top_value):
    factor_of, own = 1.0, jax.random.fold_in(key, 6)
    for dim, shards_of in cuts:
        heights = jnp.exp(jax.random.uniform(jax.random.fold_in(own, dim), (shards_of,), jnp.float32, least / len(cuts), top_value / len(cuts)))
        factor_of = factor_of * jnp.repeat(heights, extent[dim] // shards_of).reshape([-1 if axis == dim else 1 for axis in range(len(extent))])
    return factor_of


def deal_out(stream_key, own, number, rows, count, top, bound, skew):
    order = jax.random.permutation(stream_key, count)
    crowded, usual = shares(count, rows * top, bound, skew, True), shares(count, rows * top, bound, skew, False)
    places = jnp.arange(count)

    def named(tallies, rotation):
        used = int((tallies > 0).sum())
        fixed = max(1, used // 4)
        moved = fixed + (places - fixed + rotation * (used - fixed)) % max(1, count - fixed)
        return jnp.zeros((count,), jnp.int32).at[order[jnp.where(places < fixed, places, moved)]].set(jnp.asarray(tallies, jnp.int32))

    tallies = jnp.where(number % 4 == 0, named(crowded, number // 4), named(usual, number - number // 4 - 1))
    mixed = jax.random.permutation(jax.random.fold_in(own, 3), count)
    giver, receiver = mixed[0:count // 2 * 2:2], mixed[1:count // 2 * 2:2]
    slack = jnp.minimum(tallies[giver] - 1, bound - tallies[receiver]) // 2
    slack = jnp.where((giver == order[0]) | (receiver == order[0]) | (tallies[receiver] == 0), 0, jnp.maximum(slack, 0))
    moved = jax.random.randint(jax.random.fold_in(own, 4), (count // 2,), 0, 1 << 20) % (slack + 1)
    tallies = tallies.at[giver].add(-moved).at[receiver].add(moved)
    labels = jnp.searchsorted(jnp.cumsum(tallies), jnp.arange(rows * top), side="right").astype(jnp.int32)
    grid = labels.reshape(top, rows).T
    grid = grid[jax.random.permutation(jax.random.fold_in(own, 1), rows)]
    rotation = jax.random.randint(jax.random.fold_in(own, 2), (rows, 1), 0, top)
    return jnp.take_along_axis(grid, (jnp.arange(top)[None, :] + rotation) % top, axis=1)


def shares(count, total, limit, slope, full):
    weights = [(1 << 20) // math.isqrt(grade ** slope) + 1 for grade in range(1, count + 1)]
    largest = limit if full else min(limit, max(-(-total // count), total * weights[0] // sum(weights)))
    least = 1 if total - largest >= count - 1 else 0
    given, rest = [largest] + [least] * (count - 1), total - largest - least * (count - 1)
    while rest > 0:
        candidates = [i for i in range(1, count) if given[i] < largest] or [i for i in range(1, count) if given[i] < limit]
        pool, left = sum([weights[i] for i in candidates]), rest
        for i in candidates:
            extra = min(limit - given[i], max(1, left * weights[i] // pool), rest)
            given[i] = given[i] + extra
            rest = rest - extra
    return np.array(given)


def normal_values(rng, dims, spread, most, shards=(), held_as=jnp.bfloat16):
    drawn = spread * jax.random.normal(rng, dims, jnp.float32)
    if shards:
        drawn = drawn * block_scale(rng, dims, shards, -0.22, 0.18)
    return jnp.clip(drawn, -most, most).astype(held_as)


def noise_with(stream_key, extent, deviation, most, cuts, heavy, kind=jnp.bfloat16):
    drawn = deviation * jax.random.normal(stream_key, extent, jnp.float32)
    if cuts:
        drawn = drawn * block_scale(stream_key, extent, cuts, -0.22, 0.18)
    return jnp.clip(spiked(drawn, jax.random.fold_in(stream_key, 3), *heavy), -most, most).astype(kind)


def setup_inputs(seed: int = 0) -> dict:
    key_list = jax.random.split(jax.random.key(seed), 8)
    tokens = noise_with(key_list[0], (TOKENS, D), 1.0, 6.0, ((0, 32),), (0, 1, 32, 2.75))
    out_grad = normal_values(key_list[1], (TOKENS, D), 1.0, 6.0, ((0, 32),))
    routes_keys = jax.random.split(jax.random.fold_in(key_list[2], 1), TOKENS // TOK_DEV)
    routes_turns = jax.random.permutation(jax.random.fold_in(key_list[2], 3), TOKENS // TOK_DEV)
    routes = jax.vmap(lambda own, number: deal_out(jax.random.fold_in(key_list[2], 2), own, number, TOK_DEV, EXPERTS, 2, CAP, 2))(routes_keys, routes_turns).reshape((TOKENS, 2))
    gates = jnp.clip(jnp.exp(math.log(1.0) - 1.609438 * jax.random.uniform(key_list[3], (TOKENS, 2), jnp.float32) ** block_scale(key_list[3], (TOKENS, 2), ((0, 32),), -0.2, 0.2)), 0.2, 1.0)
    w_gate = normal_values(key_list[4], (EXPERTS, D, FF), D ** -0.5, 0.109375, ((0, 2), (1, 16)))
    w_up = normal_values(key_list[5], (EXPERTS, D, FF), D ** -0.5, 0.109375, ((0, 2), (1, 16)))
    w_down_t = normal_values(key_list[6], (EXPERTS, D, FF), FF ** -0.5, 0.5, ((0, 2), (1, 16)))
    return {"tokens": tokens, "out_grad": out_grad, "routes": routes, "gates": gates, "w_gate": w_gate, "w_up": w_up, "w_down_t": w_down_t}


def reference(tokens, out_grad, routes, gates, w_gate, w_up, w_down_t):
    flat_routes = routes.reshape(-1)
    flat_gates = gates.reshape(-1)
    sorted_items = jnp.argsort(flat_routes, stable=True).astype(jnp.int32)
    row_limit = DEVICES * CAP
    padded = jnp.concatenate([sorted_items, jnp.zeros((row_limit,), jnp.int32)])
    token_grad = jnp.zeros(tokens.shape, jnp.float32)
    grads_in = []
    for expert in range(EXPERTS):
        first_row = jnp.sum(flat_routes < expert).astype(jnp.int32)
        live_count = jnp.sum(flat_routes == expert).astype(jnp.int32)
        picked = lax.dynamic_slice(padded, (first_row,), (row_limit,))
        live_rows = jnp.arange(row_limit, dtype=jnp.int32) < live_count
        token_index = (picked // 2).astype(jnp.int32)
        rows_in = tokens[token_index]
        slot_gates = jnp.where(live_rows, flat_gates[picked], 0.0)
        slot_grad = (out_grad[token_index].astype(jnp.float32) * slot_gates[:, None]).astype(jnp.bfloat16)
        in_weights = jnp.concatenate([w_gate[expert], w_up[expert]], axis=1)
        gate_up = jnp.dot(rows_in, in_weights, preferred_element_type=jnp.float32)
        gate_pre = gate_up[:, :FF]
        up_pre = gate_up[:, FF:]
        sigmoid_gate = jax.nn.sigmoid(gate_pre)
        silu_gate = gate_pre * sigmoid_gate
        act_grad = jnp.dot(slot_grad, w_down_t[expert], preferred_element_type=jnp.float32)
        gate_grad = act_grad * up_pre * sigmoid_gate * (1.0 + gate_pre * (1.0 - sigmoid_gate))
        up_grad = act_grad * silu_gate
        hidden_grad = jnp.concatenate([gate_grad, up_grad], axis=1).astype(jnp.bfloat16)
        slot_input = jnp.dot(hidden_grad, in_weights.T, preferred_element_type=jnp.float32).astype(jnp.bfloat16)
        token_grad = token_grad.at[token_index].add(jnp.where(live_rows[:, None], slot_input.astype(jnp.float32), 0.0))
        grads_in.append(jnp.dot(rows_in.T, hidden_grad, preferred_element_type=jnp.float32))
    grad_scale = 1.0 / math.sqrt(TOKENS)
    stacked_in = jnp.stack(grads_in) * grad_scale
    return (token_grad.astype(jnp.bfloat16), stacked_in[:, :, :FF], stacked_in[:, :, FF:])
```

```python
import functools
import math

import jax
import jax.numpy as jnp
from jax import lax
from jax.experimental import pallas as pl
from jax.experimental.pallas import tpu as pltpu
from jax.sharding import PartitionSpec as P

EXPERTS = 8
CAP = 40
INFO = 16
F32 = jnp.float32
BF16 = jnp.bfloat16


def remote(src, dst, send, recv, e, d):
    return pltpu.make_async_remote_copy(
        src_ref=src,
        dst_ref=dst,
        send_sem=send,
        recv_sem=recv,
        device_id={"expert": e, "dp": d},
        device_id_type=pl.DeviceIdType.MESH,
    )


def when(cond, fn):
    if cond is None:
        fn()
    else:
        pl.when(cond)(fn)


class Sends:
    def __init__(self):
        self.items = []

    def start(self, cond, make):
        when(cond, lambda: make().start())
        self.items.append((cond, make))

    def finish(self):
        for cond, make in self.items:
            when(cond, lambda make=make: make().wait_send())


def barrier(e, d, n_expert, n_data):
    sem = pltpu.get_barrier_semaphore()
    for j in range(1, n_data):
        pl.semaphore_signal(
            sem,
            inc=1,
            device_id={"expert": e, "dp": lax.rem(d + j, n_data)},
            device_id_type=pl.DeviceIdType.MESH,
        )
    for j in range(1, n_expert):
        pl.semaphore_signal(
            sem,
            inc=1,
            device_id={"expert": lax.rem(e + j, n_expert), "dp": d},
            device_id_type=pl.DeviceIdType.MESH,
        )
    pl.semaphore_wait(sem, n_data - 1 + n_expert - 1)


def both(p, q):
    if p is None:
        return q
    return jnp.logical_and(p, q)


def gather(e, d, n_data, owns, block, sems, sends, midway=None):
    up_s, down_s, b_s, c_s, recv = sems
    count = n_data // 4
    a, b, c = d // 4, lax.rem(d // 2, 2), lax.rem(d, 2)
    number = len(owns)

    def index(a2, b2, c2):
        return (a2 * 2 + b2) * 2 + c2

    def make(i, src, d2, target, send):
        return remote(src, block(i, d2), send, recv.at[i, d2], e, target)

    def arrive(i, d2):
        remote(block(i, d2), block(i, d2), c_s.at[i, 0], recv.at[i, d2], e, d).wait_recv()

    def pass_on(cond, i, src, a2, up, down, slot):
        d2 = index(a2, b, c)
        if up:
            sends.start(
                both(cond, a < count - 1),
                lambda: make(i, src(), d2, index(a + 1, b, c), up_s.at[i, slot]),
            )
        if down:
            sends.start(
                both(cond, a > 0),
                lambda: make(i, src(), d2, index(a - 1, b, c), down_s.at[i, slot]),
            )
        sends.start(cond, lambda: make(i, src(), d2, index(a, 1 - b, c), b_s.at[i, a2]))
        sends.start(cond, lambda: make(i, src(), d2, index(a, b, 1 - c), c_s.at[i, a2 * 2 + b]))

    def from_b(cond, a2):
        d2 = index(a2, 1 - b, c)
        for i in range(number):
            when(cond, lambda i=i: arrive(i, d2))
            sends.start(
                cond,
                lambda i=i: make(
                    i, block(i, d2), d2, index(a, b, 1 - c), c_s.at[i, a2 * 2 + 1 - b]
                ),
            )

    for i in range(number):
        pass_on(None, i, lambda i=i: owns[i], a, True, True, 0)
    if midway is not None:
        midway()
    for step in range(1, count):
        for i in range(number):
            cond, a2 = a >= step, a - step
            d2 = index(a2, b, c)
            when(cond, lambda i=i, d2=d2: arrive(i, d2))
            pass_on(cond, i, lambda i=i, d2=d2: block(i, d2), a2, True, False, step)
            cond, a2 = a + step < count, a + step
            d2 = index(a2, b, c)
            when(cond, lambda i=i, d2=d2: arrive(i, d2))
            pass_on(cond, i, lambda i=i, d2=d2: block(i, d2), a2, False, True, step)
        if step == 1:
            from_b(None, a)
        else:
            from_b(a >= step - 1, a - step + 1)
            from_b(a + step - 1 < count, a + step - 1)
    if count == 1:
        from_b(None, a)
    else:
        from_b(a >= count - 1, a - count + 1)
        from_b(a + count - 1 < count, a + count - 1)
    for a2 in range(count):
        for b2 in range(2):
            for i in range(number):
                arrive(i, index(a2, b2, 1 - c))


def first_kernel(
    n_expert, n_data, w_in, w_dn, tok, og, info, blocks,
    all_in, all_dn, tx, ox, ix, tt,
    own_sem, up_s, down_s, b_s, c_s, recv, x_s, x_r, t_s, t_r, y_s, y_r,
):
    e, d = lax.axis_index("expert"), lax.axis_index("dp")
    width = w_in.shape[1]
    rows = tok.shape[0]

    def block(i, d2):
        return (all_in, all_dn)[i].at[:, pl.ds(d2 * width, width), :]

    def columns(e2, d2):
        return tt.at[:, pl.ds(pl.multiple_of((e2 * n_data + d2) * rows, rows), rows)]

    def half(e2):
        return tt.at[:, pl.ds(pl.multiple_of(e2 * n_data * rows, n_data * rows), n_data * rows)]

    own = [
        pltpu.make_async_copy(w_in, block(0, d), own_sem.at[0]),
        pltpu.make_async_copy(w_dn, block(1, d), own_sem.at[1]),
        pltpu.make_async_copy(tok, tx.at[e], own_sem.at[2]),
        pltpu.make_async_copy(og, ox.at[e], own_sem.at[3]),
        pltpu.make_async_copy(info, ix.at[e], own_sem.at[4]),
        pltpu.make_async_copy(blocks.at[d], columns(e, d), own_sem.at[5]),
    ]
    for copy in own:
        copy.start()
    barrier(e, d, n_expert, n_data)
    sends = Sends()
    triples = ((tok, tx), (og, ox), (info, ix))

    def midway():
        for j in range(1, n_expert):
            for i, (src, dst) in enumerate(triples):
                sends.start(
                    None,
                    lambda i=i, j=j, src=src, dst=dst: remote(
                        src, dst.at[e], x_s.at[i, j], x_r.at[i, j], lax.rem(e + j, n_expert), d
                    ),
                )
        for j in range(1, n_data):
            sends.start(
                None,
                lambda j=j: remote(
                    blocks.at[lax.rem(d + j, n_data)], columns(e, d), t_s.at[j], t_r.at[j],
                    e, lax.rem(d + j, n_data),
                ),
            )

    gather(e, d, n_data, (w_in, w_dn), block, (up_s, down_s, b_s, c_s, recv), sends, midway)
    for copy in own:
        copy.wait()
    for j in range(1, n_data):
        source = lax.rem(d - j + n_data, n_data)
        remote(columns(e, source), columns(e, source), t_s.at[j], t_r.at[j], e, source).wait_recv()
    for j in range(1, n_expert):
        sends.start(
            None,
            lambda j=j: remote(half(e), half(e), y_s.at[j], y_r.at[j], lax.rem(e + j, n_expert), d),
        )
    for j in range(1, n_expert):
        source = lax.rem(e - j + n_expert, n_expert)
        for i, (src, dst) in enumerate(triples):
            remote(src, dst.at[source], x_s.at[i, j], x_r.at[i, j], source, d).wait_recv()
        remote(half(source), half(source), y_s.at[j], y_r.at[j], source, d).wait_recv()
    sends.finish()


def second_kernel(
    n_expert, n_data, hid, ret, all_hid, rx, own_sem, up_s, down_s, b_s, c_s, recv, x_s, x_r
):
    e, d = lax.axis_index("expert"), lax.axis_index("dp")

    def block(i, d2):
        return all_hid.at[d2]

    own = [
        pltpu.make_async_copy(hid, block(0, d), own_sem.at[0]),
        pltpu.make_async_copy(ret.at[e], rx.at[e], own_sem.at[1]),
    ]
    for copy in own:
        copy.start()
    barrier(e, d, n_expert, n_data)
    sends = Sends()

    def midway():
        for j in range(1, n_expert):
            target = lax.rem(e + j, n_expert)
            sends.start(
                None,
                lambda j=j, target=target: remote(
                    ret.at[target], rx.at[e], x_s.at[j], x_r.at[j], target, d
                ),
            )

    gather(e, d, n_data, (hid,), block, (up_s, down_s, b_s, c_s, recv), sends, midway)
    for copy in own:
        copy.wait()
    for j in range(1, n_expert):
        source = lax.rem(e - j + n_expert, n_expert)
        remote(ret.at[source], rx.at[source], x_s.at[j], x_r.at[j], source, d).wait_recv()
    sends.finish()


def picker(e0, p0, e1, p1, expert, n_expert, rows):
    shape = (n_expert * CAP, n_expert * rows)
    slot = lax.broadcasted_iota(jnp.int32, shape, 0)
    base = (lax.broadcasted_iota(jnp.int32, (1, shape[1]), 1) // rows) * CAP
    want0 = jnp.where(e0 == expert, p0.astype(jnp.int32) + base, -1)
    want1 = jnp.where(e1 == expert, p1.astype(jnp.int32) + base, -1)
    hit = jnp.logical_or(slot == want0, slot == want1)
    return jnp.where(hit, 1.0, 0.0).astype(BF16)


def compute_kernel(n_expert, tx, ox, info_r, info_c, w_in, w_dn, hid, ret, acc):
    x, local_count = pl.program_id(0), pl.num_programs(0)
    hidden = w_dn.shape[2]
    rows = tx.shape[0] // n_expert
    expert = (lax.axis_index("expert") * local_count + x).astype(F32)
    gate_up = jnp.dot(tx[...], w_in[0], preferred_element_type=F32)
    back = jnp.dot(ox[...], w_dn[0], preferred_element_type=F32)
    gate = jnp.where(info_c[:, 0:1] == expert, info_c[:, 4:5], 0.0) + jnp.where(
        info_c[:, 2:3] == expert, info_c[:, 5:6], 0.0
    )
    act_grad = back * gate
    gate_pre, up_pre = gate_up[:, :hidden], gate_up[:, hidden:]
    s = jax.nn.sigmoid(gate_pre)
    gate_grad = act_grad * up_pre * s * (1.0 + gate_pre * (1.0 - s))
    up_grad = act_grad * (gate_pre * s)
    grad = jnp.concatenate([gate_grad, up_grad], axis=1).astype(BF16)
    pick = picker(
        info_r[0:1, :], info_r[1:2, :], info_r[2:3, :], info_r[3:4, :], expert, n_expert, rows
    )
    hid[0] = jnp.dot(pick, grad, preferred_element_type=F32).astype(BF16)
    term = lax.dot_general(grad, w_in[0], (((1,), (1,)), ((), ())), preferred_element_type=F32)

    @pl.when(x == 0)
    def _():
        acc[...] = term

    @pl.when(x > 0)
    def _():
        acc[...] += term

    @pl.when(x == local_count - 1)
    def _():
        ret[...] = acc[...].astype(BF16)


def grad_kernel(n_expert, local_count, scale, *refs):
    tts, (hid, out_g, out_u) = refs[:n_expert], refs[n_expert:]
    step, steps = pl.program_id(0), pl.num_programs(0)
    width, hidden = out_g.shape[1], out_g.shape[2]
    rows = tts[0].shape[1]
    tok = jnp.concatenate([t[:width, :] for t in tts], axis=1)
    info = jnp.concatenate([t[width:, :] for t in tts], axis=1).astype(F32)

    @pl.when(step == 0)
    def _():
        out_g[...] = jnp.zeros_like(out_g)
        out_u[...] = jnp.zeros_like(out_u)

    for x in range(local_count):
        expert = (lax.axis_index("expert") * local_count + x).astype(F32)
        pick = picker(info[0:1], info[1:2], info[2:3], info[3:4], expert, n_expert, rows)
        got = lax.dot_general(
            tok, pick, (((1,), (1,)), ((), ())), preferred_element_type=F32
        ).astype(BF16)
        term = jnp.dot(got, hid[0, x], preferred_element_type=F32) * scale
        out_g[x] += term[:, :hidden]
        out_u[x] += term[:, hidden:]


def local(tokens, out_grad, routes, gates, w_gate, w_up, w_down_t):
    rows, model = tokens.shape
    n_expert = lax.axis_size("expert")
    n_data = lax.axis_size("dp")
    local_count, width, hidden = w_gate.shape
    count = n_data // 4
    any_, vmem = pl.BlockSpec(memory_space=pl.ANY), pl.BlockSpec(memory_space=pltpu.VMEM)
    dma = pltpu.SemaphoreType.DMA

    flat = routes.reshape(-1)
    onehot = (flat[:, None] == jnp.arange(EXPERTS, dtype=jnp.int32)[None, :]).astype(jnp.int32)
    position = jnp.sum((jnp.cumsum(onehot, axis=0) - 1) * onehot, axis=1).reshape(rows, 2)
    info = jnp.stack(
        [
            routes[:, 0].astype(F32), position[:, 0].astype(F32),
            routes[:, 1].astype(F32), position[:, 1].astype(F32),
            gates[:, 0], gates[:, 1], gates[:, 0], gates[:, 1],
        ]
    )
    side = jnp.concatenate([info[:4].astype(BF16), jnp.zeros((INFO - 4, rows), BF16)], axis=0)
    blocks = jnp.concatenate(
        [
            tokens.T.reshape(n_data, width, rows),
            jnp.broadcast_to(side[None], (n_data, INFO, rows)),
        ],
        axis=1,
    )
    w_in = jnp.concatenate([w_gate, w_up], axis=2)

    def chain_sems(number):
        return [
            dma((number, count)), dma((number, count)), dma((number, count)),
            dma((number, 2 * count)), dma((number, n_data)),
        ]

    shape = jax.ShapeDtypeStruct
    all_in, all_dn, tx, ox, ix, tt = pl.pallas_call(
        functools.partial(first_kernel, n_expert, n_data),
        out_shape=(
            shape((local_count, model, 2 * hidden), BF16),
            shape((local_count, model, hidden), BF16),
            shape((n_expert, rows, model), BF16),
            shape((n_expert, rows, model), BF16),
            shape((n_expert, 8, rows), F32),
            shape((width + INFO, n_expert * n_data * rows), BF16),
        ),
        in_specs=[vmem] * 6,
        out_specs=[any_] * 6,
        scratch_shapes=[dma((6,))]
        + chain_sems(2)
        + [
            dma((3, n_expert)), dma((3, n_expert)), dma((n_data,)), dma((n_data,)),
            dma((n_expert,)), dma((n_expert,)),
        ],
        compiler_params=pltpu.CompilerParams(collective_id=0, has_side_effects=True),
    )(w_in, w_down_t, tokens, out_grad, info, blocks)

    info_r = jnp.transpose(ix, (1, 0, 2)).reshape(8, n_expert * rows)
    info_c = info_r.T
    total = n_expert * rows
    slots = n_expert * CAP
    hid, ret = pl.pallas_call(
        functools.partial(compute_kernel, n_expert),
        grid=(local_count,),
        out_shape=(shape((local_count, slots, 2 * hidden), BF16), shape((total, model), BF16)),
        in_specs=[
            pl.BlockSpec((total, model), lambda x: (0, 0)),
            pl.BlockSpec((total, model), lambda x: (0, 0)),
            pl.BlockSpec((8, total), lambda x: (0, 0)),
            pl.BlockSpec((total, 8), lambda x: (0, 0)),
            pl.BlockSpec((1, model, 2 * hidden), lambda x: (x, 0, 0)),
            pl.BlockSpec((1, model, hidden), lambda x: (x, 0, 0)),
        ],
        out_specs=[
            pl.BlockSpec((1, slots, 2 * hidden), lambda x: (x, 0, 0)),
            pl.BlockSpec((total, model), lambda x: (0, 0)),
        ],
        scratch_shapes=[pltpu.VMEM((total, model), F32)],
        compiler_params=pltpu.CompilerParams(vmem_limit_bytes=60 * 1024 * 1024),
    )(tx.reshape(total, model), ox.reshape(total, model), info_r, info_c, all_in, all_dn)

    all_hid, rx = pl.pallas_call(
        functools.partial(second_kernel, n_expert, n_data),
        out_shape=(
            shape((n_data, local_count, slots, 2 * hidden), BF16),
            shape((n_expert, rows, model), BF16),
        ),
        in_specs=[vmem] * 2,
        out_specs=[any_] * 2,
        scratch_shapes=[dma((2,))] + chain_sems(1) + [dma((n_expert,)), dma((n_expert,))],
        compiler_params=pltpu.CompilerParams(collective_id=1, has_side_effects=True),
    )(hid, ret.reshape(n_expert, rows, model))

    token_grad = jnp.sum(rx.astype(F32), axis=0).astype(BF16)
    grad_scale = 1.0 / math.sqrt(rows * n_expert * n_data)

    def tt_spec(s):
        return pl.BlockSpec((width + INFO, rows), lambda i: (0, s * n_data + i))

    grad_gate, grad_up = pl.pallas_call(
        functools.partial(grad_kernel, n_expert, local_count, grad_scale),
        grid=(n_data,),
        out_shape=(
            shape((local_count, width, hidden), F32),
            shape((local_count, width, hidden), F32),
        ),
        in_specs=[tt_spec(s) for s in range(n_expert)]
        + [pl.BlockSpec((1, local_count, slots, 2 * hidden), lambda i: (i, 0, 0, 0))],
        out_specs=[pl.BlockSpec((local_count, width, hidden), lambda i: (0, 0, 0))] * 2,
    )(*([tt] * n_expert), all_hid)
    return token_grad, grad_gate, grad_up


def solution(mesh):
    row, split = P(("expert", "dp"), None), P("expert", "dp", None)
    return jax.shard_map(
        local,
        mesh=mesh,
        in_specs=(row, row, row, row, split, split, split),
        out_specs=(row, split, split),
        check_vma=False,
    )
```

```python
import functools
import math

import jax
import jax.numpy as jnp
from jax import lax
from jax.experimental import pallas as pl
from jax.experimental.pallas import tpu as pltpu
from jax.sharding import PartitionSpec as P

EXPERTS = 8
CAP = 40
INFO = 16
F32 = jnp.float32
BF16 = jnp.bfloat16


def remote(src, dst, send, recv, e, d):
    return pltpu.make_async_remote_copy(
        src_ref=src,
        dst_ref=dst,
        send_sem=send,
        recv_sem=recv,
        device_id={"expert": e, "dp": d},
        device_id_type=pl.DeviceIdType.MESH,
    )


def when(cond, fn):
    if cond is None:
        fn()
    else:
        pl.when(cond)(fn)


class Sends:
    def __init__(self):
        self.items = []

    def start(self, cond, make):
        when(cond, lambda: make().start())
        self.items.append((cond, make))

    def finish(self):
        for cond, make in self.items:
            when(cond, lambda make=make: make().wait_send())


def barrier(e, d, n_expert, n_data):
    sem = pltpu.get_barrier_semaphore()
    for j in range(1, n_data):
        pl.semaphore_signal(
            sem,
            inc=1,
            device_id={"expert": e, "dp": lax.rem(d + j, n_data)},
            device_id_type=pl.DeviceIdType.MESH,
        )
    for j in range(1, n_expert):
        pl.semaphore_signal(
            sem,
            inc=1,
            device_id={"expert": lax.rem(e + j, n_expert), "dp": d},
            device_id_type=pl.DeviceIdType.MESH,
        )
    pl.semaphore_wait(sem, n_data - 1 + n_expert - 1)


def both(p, q):
    if p is None:
        return q
    return jnp.logical_and(p, q)


def gather(e, d, n_data, owns, block, sems, sends, hook=None, use=None):
    up_s, down_s, b_s, c_s, recv = sems
    count = n_data // 4
    a, b, c = d // 4, lax.rem(d // 2, 2), lax.rem(d, 2)
    number = len(owns)

    def index(a2, b2, c2):
        return (a2 * 2 + b2) * 2 + c2

    def make(i, src, d2, target, send):
        return remote(src, block(i, d2), send, recv.at[i, d2], e, target)

    def arrive(i, d2):
        remote(block(i, d2), block(i, d2), c_s.at[i, 0], recv.at[i, d2], e, d).wait_recv()

    def pass_on(cond, i, src, a2, up, down, slot):
        d2 = index(a2, b, c)
        if up:
            sends.start(
                both(cond, a < count - 1),
                lambda: make(i, src(), d2, index(a + 1, b, c), up_s.at[i, slot]),
            )
        if down:
            sends.start(
                both(cond, a > 0),
                lambda: make(i, src(), d2, index(a - 1, b, c), down_s.at[i, slot]),
            )
        sends.start(cond, lambda: make(i, src(), d2, index(a, 1 - b, c), b_s.at[i, a2]))
        sends.start(cond, lambda: make(i, src(), d2, index(a, b, 1 - c), c_s.at[i, a2 * 2 + b]))

    def from_b(cond, a2):
        d2 = index(a2, 1 - b, c)
        for i in range(number):
            when(cond, lambda i=i: arrive(i, d2))
            sends.start(
                cond,
                lambda i=i: make(
                    i, block(i, d2), d2, index(a, b, 1 - c), c_s.at[i, a2 * 2 + 1 - b]
                ),
            )

    for step in range(count + 2):
        if step == 0:
            for i in range(number):
                pass_on(None, i, lambda i=i: owns[i], a, True, True, 0)
        elif step < count:
            for i in range(number):
                cond, a2 = a >= step, a - step
                d2 = index(a2, b, c)
                when(cond, lambda i=i, d2=d2: arrive(i, d2))
                pass_on(cond, i, lambda i=i, d2=d2: block(i, d2), a2, True, False, step)
                cond, a2 = a + step < count, a + step
                d2 = index(a2, b, c)
                when(cond, lambda i=i, d2=d2: arrive(i, d2))
                pass_on(cond, i, lambda i=i, d2=d2: block(i, d2), a2, False, True, step)
        if step == 1:
            from_b(None, a)
        elif 1 < step <= count:
            from_b(a >= step - 1, a - step + 1)
            from_b(a + step - 1 < count, a + step - 1)
        if hook is not None:
            hook(step, count)

        def job(j, carry, step=step):
            flip_b, flip_c, way = lax.rem(j // 2, 2), j // 4, lax.rem(j, 2)
            shift = step - flip_b - flip_c
            a2 = a - shift + 2 * shift * way
            d2 = index(a2, b + flip_b * (1 - 2 * b), c + flip_c * (1 - 2 * c))
            far = jnp.logical_or(shift > 0, jnp.logical_and(shift == 0, way == 0))
            valid = jnp.logical_and(far, jnp.logical_and(a2 >= 0, a2 < count))

            @pl.when(jnp.logical_and(valid, flip_c == 1))
            def _():
                for i in range(number):
                    arrive(i, d2)

            if use is not None:
                pl.when(valid)(lambda: use(d2))
            return carry

        lax.fori_loop(0, 8, job, 0)


def first_kernel(
    n_expert, n_data, w_in, w_dn, tok, og, info, blocks,
    all_in, all_dn, tx, ox, ix, tt,
    own_sem, up_s, down_s, b_s, c_s, recv, x_s, x_r, t_s, t_r, y_s, y_r,
):
    e, d = lax.axis_index("expert"), lax.axis_index("dp")
    width = w_in.shape[1]
    rows = tok.shape[0]

    def block(i, d2):
        return (all_in, all_dn)[i].at[:, pl.ds(d2 * width, width), :]

    def columns(e2, d2):
        return tt.at[:, pl.ds(pl.multiple_of((e2 * n_data + d2) * rows, rows), rows)]

    def half(e2):
        return tt.at[:, pl.ds(pl.multiple_of(e2 * n_data * rows, n_data * rows), n_data * rows)]

    own = [
        pltpu.make_async_copy(w_in, block(0, d), own_sem.at[0]),
        pltpu.make_async_copy(w_dn, block(1, d), own_sem.at[1]),
        pltpu.make_async_copy(tok, tx.at[e], own_sem.at[2]),
        pltpu.make_async_copy(og, ox.at[e], own_sem.at[3]),
        pltpu.make_async_copy(info, ix.at[e], own_sem.at[4]),
        pltpu.make_async_copy(blocks.at[d], columns(e, d), own_sem.at[5]),
    ]
    for copy in own:
        copy.start()
    barrier(e, d, n_expert, n_data)
    sends = Sends()
    triples = ((tok, tx), (og, ox), (info, ix))

    def hook(step, count):
        if step == count - 1:
            relay()
        if step > 0:
            return
        for j in range(1, n_expert):
            for i, (src, dst) in enumerate(triples):
                sends.start(
                    None,
                    lambda i=i, j=j, src=src, dst=dst: remote(
                        src, dst.at[e], x_s.at[i, j], x_r.at[i, j], lax.rem(e + j, n_expert), d
                    ),
                )
        for j in range(1, n_data):
            sends.start(
                None,
                lambda j=j: remote(
                    blocks.at[lax.rem(d + j, n_data)], columns(e, d), t_s.at[j], t_r.at[j],
                    e, lax.rem(d + j, n_data),
                ),
            )

    def relay():
        own[5].wait()
        for j in range(1, n_data):
            source = lax.rem(d - j + n_data, n_data)
            place = columns(e, source)
            remote(place, place, t_s.at[j], t_r.at[j], e, source).wait_recv()
        for j in range(1, n_expert):
            sends.start(
                None,
                lambda j=j: remote(
                    half(e), half(e), y_s.at[j], y_r.at[j], lax.rem(e + j, n_expert), d
                ),
            )

    gather(e, d, n_data, (w_in, w_dn), block, (up_s, down_s, b_s, c_s, recv), sends, hook)
    for copy in own[:5]:
        copy.wait()
    for j in range(1, n_expert):
        source = lax.rem(e - j + n_expert, n_expert)
        for i, (src, dst) in enumerate(triples):
            remote(src, dst.at[source], x_s.at[i, j], x_r.at[i, j], source, d).wait_recv()
        remote(half(source), half(source), y_s.at[j], y_r.at[j], source, d).wait_recv()
    sends.finish()


def second_kernel(
    n_expert, n_data, scale, hid, ret, tt, rx, out_g, out_u,
    all_hid, own_sem, up_s, down_s, b_s, c_s, recv, x_s, x_r,
):
    e, d = lax.axis_index("expert"), lax.axis_index("dp")
    local_count, width, hidden = out_g.shape
    rows = tt.shape[1] // (n_expert * n_data)

    def block(i, d2):
        return all_hid.at[d2]

    own = [
        pltpu.make_async_copy(hid, block(0, d), own_sem.at[0]),
        pltpu.make_async_copy(ret.at[e], rx.at[e], own_sem.at[1]),
    ]
    for copy in own:
        copy.start()
    barrier(e, d, n_expert, n_data)
    sends = Sends()

    def hook(step, count):
        if step > 0:
            return
        for j in range(1, n_expert):
            target = lax.rem(e + j, n_expert)
            sends.start(
                None,
                lambda j=j, target=target: remote(
                    ret.at[target], rx.at[e], x_s.at[j], x_r.at[j], target, d
                ),
            )
        out_g[...] = jnp.zeros_like(out_g)
        out_u[...] = jnp.zeros_like(out_u)
        own[0].wait()

    def use(d2):
        parts = [
            tt[:, pl.ds(pl.multiple_of((s * n_data + d2) * rows, rows), rows)]
            for s in range(n_expert)
        ]
        both_tt = jnp.concatenate(parts, axis=1)
        tok, info = both_tt[:width], both_tt[width:].astype(F32)
        for x in range(local_count):
            expert = (e * local_count + x).astype(F32)
            pick = picker(info[0:1], info[1:2], info[2:3], info[3:4], expert, n_expert, rows)
            got = lax.dot_general(
                tok, pick, (((1,), (1,)), ((), ())), preferred_element_type=F32
            ).astype(BF16)
            term = jnp.dot(got, all_hid[d2, x], preferred_element_type=F32) * scale
            out_g[x] += term[:, :hidden]
            out_u[x] += term[:, hidden:]

    gather(e, d, n_data, (hid,), block, (up_s, down_s, b_s, c_s, recv), sends, hook, use)
    own[1].wait()
    for j in range(1, n_expert):
        source = lax.rem(e - j + n_expert, n_expert)
        remote(ret.at[source], rx.at[source], x_s.at[j], x_r.at[j], source, d).wait_recv()
    sends.finish()


def picker(e0, p0, e1, p1, expert, n_expert, rows):
    shape = (n_expert * CAP, n_expert * rows)
    slot = lax.broadcasted_iota(jnp.int32, shape, 0)
    base = (lax.broadcasted_iota(jnp.int32, (1, shape[1]), 1) // rows) * CAP
    want0 = jnp.where(e0 == expert, p0.astype(jnp.int32) + base, -1)
    want1 = jnp.where(e1 == expert, p1.astype(jnp.int32) + base, -1)
    hit = jnp.logical_or(slot == want0, slot == want1)
    return jnp.where(hit, 1.0, 0.0).astype(BF16)


def compute_kernel(n_expert, tx, ox, info_r, info_c, w_in, w_dn, hid, ret, acc):
    x, local_count = pl.program_id(0), pl.num_programs(0)
    hidden = w_dn.shape[2]
    rows = tx.shape[0] // n_expert
    expert = (lax.axis_index("expert") * local_count + x).astype(F32)
    gate_up = jnp.dot(tx[...], w_in[0], preferred_element_type=F32)
    back = jnp.dot(ox[...], w_dn[0], preferred_element_type=F32)
    gate = jnp.where(info_c[:, 0:1] == expert, info_c[:, 4:5], 0.0) + jnp.where(
        info_c[:, 2:3] == expert, info_c[:, 5:6], 0.0
    )
    act_grad = back * gate
    gate_pre, up_pre = gate_up[:, :hidden], gate_up[:, hidden:]
    s = jax.nn.sigmoid(gate_pre)
    gate_grad = act_grad * up_pre * s * (1.0 + gate_pre * (1.0 - s))
    up_grad = act_grad * (gate_pre * s)
    grad = jnp.concatenate([gate_grad, up_grad], axis=1).astype(BF16)
    pick = picker(
        info_r[0:1, :], info_r[1:2, :], info_r[2:3, :], info_r[3:4, :], expert, n_expert, rows
    )
    hid[0] = jnp.dot(pick, grad, preferred_element_type=F32).astype(BF16)
    term = lax.dot_general(grad, w_in[0], (((1,), (1,)), ((), ())), preferred_element_type=F32)

    @pl.when(x == 0)
    def _():
        acc[...] = term

    @pl.when(x > 0)
    def _():
        acc[...] += term

    @pl.when(x == local_count - 1)
    def _():
        ret[...] = acc[...].astype(BF16)


def local(tokens, out_grad, routes, gates, w_gate, w_up, w_down_t):
    rows, model = tokens.shape
    n_expert = lax.axis_size("expert")
    n_data = lax.axis_size("dp")
    local_count, width, hidden = w_gate.shape
    count = n_data // 4
    any_, vmem = pl.BlockSpec(memory_space=pl.ANY), pl.BlockSpec(memory_space=pltpu.VMEM)
    dma = pltpu.SemaphoreType.DMA

    flat = routes.reshape(-1)
    onehot = (flat[:, None] == jnp.arange(EXPERTS, dtype=jnp.int32)[None, :]).astype(jnp.int32)
    position = jnp.sum((jnp.cumsum(onehot, axis=0) - 1) * onehot, axis=1).reshape(rows, 2)
    info = jnp.stack(
        [
            routes[:, 0].astype(F32), position[:, 0].astype(F32),
            routes[:, 1].astype(F32), position[:, 1].astype(F32),
            gates[:, 0], gates[:, 1], gates[:, 0], gates[:, 1],
        ]
    )
    side = jnp.concatenate([info[:4].astype(BF16), jnp.zeros((INFO - 4, rows), BF16)], axis=0)
    blocks = jnp.concatenate(
        [
            tokens.T.reshape(n_data, width, rows),
            jnp.broadcast_to(side[None], (n_data, INFO, rows)),
        ],
        axis=1,
    )
    w_in = jnp.concatenate([w_gate, w_up], axis=2)

    def chain_sems(number):
        return [
            dma((number, count)), dma((number, count)), dma((number, count)),
            dma((number, 2 * count)), dma((number, n_data)),
        ]

    shape = jax.ShapeDtypeStruct
    all_in, all_dn, tx, ox, ix, tt = pl.pallas_call(
        functools.partial(first_kernel, n_expert, n_data),
        out_shape=(
            shape((local_count, model, 2 * hidden), BF16),
            shape((local_count, model, hidden), BF16),
            shape((n_expert, rows, model), BF16),
            shape((n_expert, rows, model), BF16),
            shape((n_expert, 8, rows), F32),
            shape((width + INFO, n_expert * n_data * rows), BF16),
        ),
        in_specs=[vmem] * 6,
        out_specs=[any_] * 6,
        scratch_shapes=[dma((6,))]
        + chain_sems(2)
        + [
            dma((3, n_expert)), dma((3, n_expert)), dma((n_data,)), dma((n_data,)),
            dma((n_expert,)), dma((n_expert,)),
        ],
        compiler_params=pltpu.CompilerParams(collective_id=0, has_side_effects=True),
    )(w_in, w_down_t, tokens, out_grad, info, blocks)

    info_r = jnp.transpose(ix, (1, 0, 2)).reshape(8, n_expert * rows)
    info_c = info_r.T
    total = n_expert * rows
    slots = n_expert * CAP
    hid, ret = pl.pallas_call(
        functools.partial(compute_kernel, n_expert),
        grid=(local_count,),
        out_shape=(shape((local_count, slots, 2 * hidden), BF16), shape((total, model), BF16)),
        in_specs=[
            pl.BlockSpec((total, model), lambda x: (0, 0)),
            pl.BlockSpec((total, model), lambda x: (0, 0)),
            pl.BlockSpec((8, total), lambda x: (0, 0)),
            pl.BlockSpec((total, 8), lambda x: (0, 0)),
            pl.BlockSpec((1, model, 2 * hidden), lambda x: (x, 0, 0)),
            pl.BlockSpec((1, model, hidden), lambda x: (x, 0, 0)),
        ],
        out_specs=[
            pl.BlockSpec((1, slots, 2 * hidden), lambda x: (x, 0, 0)),
            pl.BlockSpec((total, model), lambda x: (0, 0)),
        ],
        scratch_shapes=[pltpu.VMEM((total, model), F32)],
        compiler_params=pltpu.CompilerParams(vmem_limit_bytes=60 * 1024 * 1024),
    )(tx.reshape(total, model), ox.reshape(total, model), info_r, info_c, all_in, all_dn)

    grad_scale = 1.0 / math.sqrt(rows * n_expert * n_data)
    rx, grad_gate, grad_up = pl.pallas_call(
        functools.partial(second_kernel, n_expert, n_data, grad_scale),
        out_shape=(
            shape((n_expert, rows, model), BF16),
            shape((local_count, width, hidden), F32),
            shape((local_count, width, hidden), F32),
        ),
        in_specs=[vmem] * 3,
        out_specs=[any_, vmem, vmem],
        scratch_shapes=[pltpu.VMEM((n_data, local_count, slots, 2 * hidden), BF16), dma((2,))]
        + chain_sems(1)
        + [dma((n_expert,)), dma((n_expert,))],
        compiler_params=pltpu.CompilerParams(
            collective_id=1, has_side_effects=True, vmem_limit_bytes=60 * 1024 * 1024
        ),
    )(hid, ret.reshape(n_expert, rows, model), tt)
    token_grad = jnp.sum(rx.astype(F32), axis=0).astype(BF16)
    return token_grad, grad_gate, grad_up


def solution(mesh):
    row, split = P(("expert", "dp"), None), P("expert", "dp", None)
    return jax.shard_map(
        local,
        mesh=mesh,
        in_specs=(row, row, row, row, split, split, split),
        out_specs=(row, split, split),
        check_vma=False,
    )
```

```python
import functools
import math

import jax
import jax.numpy as jnp
from jax import lax
from jax.experimental import pallas as pl
from jax.experimental.pallas import tpu as pltpu
from jax.sharding import PartitionSpec as P

EXPERTS = 8
CAP = 40
INFO = 16
F32 = jnp.float32
BF16 = jnp.bfloat16


def remote(src, dst, send, recv, e, d):
    return pltpu.make_async_remote_copy(
        src_ref=src,
        dst_ref=dst,
        send_sem=send,
        recv_sem=recv,
        device_id={"expert": e, "dp": d},
        device_id_type=pl.DeviceIdType.MESH,
    )


def when(cond, fn):
    if cond is None:
        fn()
    else:
        pl.when(cond)(fn)


class Sends:
    def __init__(self):
        self.items = []

    def start(self, cond, make):
        when(cond, lambda: make().start())
        self.items.append((cond, make))

    def finish(self):
        for cond, make in self.items:
            when(cond, lambda make=make: make().wait_send())


def barrier(e, d, n_expert, n_data):
    sem = pltpu.get_barrier_semaphore()
    for j in range(1, n_data):
        pl.semaphore_signal(
            sem,
            inc=1,
            device_id={"expert": e, "dp": lax.rem(d + j, n_data)},
            device_id_type=pl.DeviceIdType.MESH,
        )
    for j in range(1, n_expert):
        pl.semaphore_signal(
            sem,
            inc=1,
            device_id={"expert": lax.rem(e + j, n_expert), "dp": d},
            device_id_type=pl.DeviceIdType.MESH,
        )
    pl.semaphore_wait(sem, n_data - 1 + n_expert - 1)


def both(p, q):
    if p is None:
        return q
    return jnp.logical_and(p, q)


def gather(e, d, n_data, owns, block, sems, sends, hook=None, use=None):
    up_s, down_s, b_s, c_s, recv = sems
    count = n_data // 4
    a, b, c = d // 4, lax.rem(d // 2, 2), lax.rem(d, 2)
    number = len(owns)

    def index(a2, b2, c2):
        return (a2 * 2 + b2) * 2 + c2

    def make(i, src, d2, target, send):
        return remote(src, block(i, d2), send, recv.at[i, d2], e, target)

    def arrive(i, d2):
        remote(block(i, d2), block(i, d2), c_s.at[i, 0], recv.at[i, d2], e, d).wait_recv()

    def pass_on(cond, i, src, a2, up, down, slot):
        d2 = index(a2, b, c)
        if up:
            sends.start(
                both(cond, a < count - 1),
                lambda: make(i, src(), d2, index(a + 1, b, c), up_s.at[i, slot]),
            )
        if down:
            sends.start(
                both(cond, a > 0),
                lambda: make(i, src(), d2, index(a - 1, b, c), down_s.at[i, slot]),
            )
        sends.start(cond, lambda: make(i, src(), d2, index(a, 1 - b, c), b_s.at[i, a2]))
        sends.start(cond, lambda: make(i, src(), d2, index(a, b, 1 - c), c_s.at[i, a2 * 2 + b]))

    def from_b(cond, a2):
        d2 = index(a2, 1 - b, c)
        for i in range(number):
            when(cond, lambda i=i: arrive(i, d2))
            sends.start(
                cond,
                lambda i=i: make(
                    i, block(i, d2), d2, index(a, b, 1 - c), c_s.at[i, a2 * 2 + 1 - b]
                ),
            )

    for step in range(count + 2):
        if step == 0:
            for i in range(number):
                pass_on(None, i, lambda i=i: owns[i], a, True, True, 0)
        elif step < count:
            for i in range(number):
                cond, a2 = a >= step, a - step
                d2 = index(a2, b, c)
                when(cond, lambda i=i, d2=d2: arrive(i, d2))
                pass_on(cond, i, lambda i=i, d2=d2: block(i, d2), a2, True, False, step)
                cond, a2 = a + step < count, a + step
                d2 = index(a2, b, c)
                when(cond, lambda i=i, d2=d2: arrive(i, d2))
                pass_on(cond, i, lambda i=i, d2=d2: block(i, d2), a2, False, True, step)
        if step == 1:
            from_b(None, a)
        elif 1 < step <= count:
            from_b(a >= step - 1, a - step + 1)
            from_b(a + step - 1 < count, a + step - 1)
        if hook is not None:
            hook(step, count)

        def job(j, carry, step=step):
            flip_b, flip_c, way = lax.rem(j // 2, 2), j // 4, lax.rem(j, 2)
            shift = step - flip_b - flip_c
            a2 = a - shift + 2 * shift * way
            d2 = index(a2, b + flip_b * (1 - 2 * b), c + flip_c * (1 - 2 * c))
            far = jnp.logical_or(shift > 0, jnp.logical_and(shift == 0, way == 0))
            valid = jnp.logical_and(far, jnp.logical_and(a2 >= 0, a2 < count))

            @pl.when(jnp.logical_and(valid, flip_c == 1))
            def _():
                for i in range(number):
                    arrive(i, d2)

            if use is not None:
                pl.when(valid)(lambda: use(d2))
            return carry

        lax.fori_loop(0, 8, job, 0)


def first_kernel(
    n_expert, n_data, w_g, w_u, w_dn, tok, og, info, blocks,
    all_g, all_u, all_dn, tx, ox, ix, tt,
    own_sem, up_s, down_s, b_s, c_s, recv, x_s, x_r, t_s, t_r, y_s, y_r,
):
    e, d = lax.axis_index("expert"), lax.axis_index("dp")
    width = w_g.shape[1]
    rows = tok.shape[0]

    def block(i, d2):
        return (all_g, all_u, all_dn)[i].at[:, pl.ds(d2 * width, width), :]

    def columns(e2, d2):
        return tt.at[:, pl.ds(pl.multiple_of((e2 * n_data + d2) * rows, rows), rows)]

    def half(e2):
        return tt.at[:, pl.ds(pl.multiple_of(e2 * n_data * rows, n_data * rows), n_data * rows)]

    own = [
        pltpu.make_async_copy(w_g, block(0, d), own_sem.at[0]),
        pltpu.make_async_copy(w_dn, block(2, d), own_sem.at[1]),
        pltpu.make_async_copy(tok, tx.at[e], own_sem.at[2]),
        pltpu.make_async_copy(og, ox.at[e], own_sem.at[3]),
        pltpu.make_async_copy(info, ix.at[e], own_sem.at[4]),
        pltpu.make_async_copy(blocks.at[d], columns(e, d), own_sem.at[5]),
        pltpu.make_async_copy(w_u, block(1, d), own_sem.at[6]),
    ]
    for copy in own:
        copy.start()
    barrier(e, d, n_expert, n_data)
    sends = Sends()
    triples = ((tok, tx), (og, ox), (info, ix))

    def hook(step, count):
        if step == 0:
            spread()
        if step == max(count - 2, 0):
            relay()

    def spread():
        for j in range(1, n_expert):
            for i, (src, dst) in enumerate(triples):
                sends.start(
                    None,
                    lambda i=i, j=j, src=src, dst=dst: remote(
                        src, dst.at[e], x_s.at[i, j], x_r.at[i, j], lax.rem(e + j, n_expert), d
                    ),
                )
        for j in range(1, n_data):
            sends.start(
                None,
                lambda j=j: remote(
                    blocks.at[lax.rem(d + j, n_data)], columns(e, d), t_s.at[j], t_r.at[j],
                    e, lax.rem(d + j, n_data),
                ),
            )

    def relay():
        own[5].wait()
        for j in range(1, n_data):
            source = lax.rem(d - j + n_data, n_data)
            place = columns(e, source)
            remote(place, place, t_s.at[j], t_r.at[j], e, source).wait_recv()
        for j in range(1, n_expert):
            sends.start(
                None,
                lambda j=j: remote(
                    half(e), half(e), y_s.at[j], y_r.at[j], lax.rem(e + j, n_expert), d
                ),
            )

    gather(e, d, n_data, (w_g, w_u, w_dn), block, (up_s, down_s, b_s, c_s, recv), sends, hook)
    for copy in own[:5] + own[6:]:
        copy.wait()
    for j in range(1, n_expert):
        source = lax.rem(e - j + n_expert, n_expert)
        for i, (src, dst) in enumerate(triples):
            remote(src, dst.at[source], x_s.at[i, j], x_r.at[i, j], source, d).wait_recv()
        remote(half(source), half(source), y_s.at[j], y_r.at[j], source, d).wait_recv()
    sends.finish()


def second_kernel(
    n_expert, n_data, hid, ret, tt, tg, out_g, out_u,
    all_hid, rx, own_sem, up_s, down_s, b_s, c_s, recv, x_s, x_r,
):
    e, d = lax.axis_index("expert"), lax.axis_index("dp")
    local_count, width, hidden = out_g.shape
    rows = tt.shape[1] // (n_expert * n_data)

    def block(i, d2):
        return all_hid.at[d2]

    own = pltpu.make_async_copy(hid, block(0, d), own_sem)
    own.start()
    barrier(e, d, n_expert, n_data)
    sends = Sends()

    def hook(step, count):
        if step > 0:
            return
        for j in range(1, n_expert):
            target = lax.rem(e + j, n_expert)
            sends.start(
                None,
                lambda j=j, target=target: remote(
                    ret.at[target], rx.at[e], x_s.at[j], x_r.at[j], target, d
                ),
            )
        out_g[...] = jnp.zeros_like(out_g)
        out_u[...] = jnp.zeros_like(out_u)
        own.wait()

    def use(d2):
        parts = [
            tt[:, pl.ds(pl.multiple_of((s * n_data + d2) * rows, rows), rows)]
            for s in range(n_expert)
        ]
        both_tt = jnp.concatenate(parts, axis=1)
        tok, info = both_tt[:width], both_tt[width:].astype(F32)
        for x in range(local_count):
            expert = (e * local_count + x).astype(F32)
            pick = picker(info[0:1], info[1:2], info[2:3], info[3:4], expert, n_expert, rows)
            got = lax.dot_general(
                tok, pick, (((1,), (1,)), ((), ())), preferred_element_type=F32
            ).astype(BF16)
            term = jnp.dot(got, all_hid[d2, x], preferred_element_type=F32)
            out_g[x] += term[:, :hidden]
            out_u[x] += term[:, hidden:]

    gather(e, d, n_data, (hid,), block, (up_s, down_s, b_s, c_s, recv), sends, hook, use)
    total = ret[e].astype(F32)
    for j in range(1, n_expert):
        source = lax.rem(e - j + n_expert, n_expert)
        remote(ret.at[source], rx.at[source], x_s.at[j], x_r.at[j], source, d).wait_recv()
        total += rx[source].astype(F32)
    tg[...] = total.astype(BF16)
    sends.finish()


def picker(e0, p0, e1, p1, expert, n_expert, rows):
    shape = (n_expert * CAP, n_expert * rows)
    slot = lax.broadcasted_iota(jnp.int32, shape, 0)
    base = (lax.broadcasted_iota(jnp.int32, (1, shape[1]), 1) // rows) * CAP
    want0 = jnp.where(e0 == expert, p0.astype(jnp.int32) + base, -1)
    want1 = jnp.where(e1 == expert, p1.astype(jnp.int32) + base, -1)
    hit = jnp.logical_or(slot == want0, slot == want1)
    return jnp.where(hit, 1.0, 0.0).astype(BF16)


def compute_kernel(n_expert, tx, ox, ix, w_g, w_u, w_dn, hid, ret, acc):
    x, local_count = pl.program_id(0), pl.num_programs(0)
    hidden = w_dn.shape[2]
    rows = tx.shape[0] // n_expert
    expert = (lax.axis_index("expert") * local_count + x).astype(F32)
    info_r = jnp.concatenate([ix[s] for s in range(n_expert)], axis=1)
    info_c = info_r.T
    w_in = jnp.concatenate([w_g[0], w_u[0]], axis=1)
    gate_up = jnp.dot(tx[...], w_in, preferred_element_type=F32)
    back = jnp.dot(ox[...], w_dn[0], preferred_element_type=F32)
    gate = jnp.where(info_c[:, 0:1] == expert, info_c[:, 4:5], 0.0) + jnp.where(
        info_c[:, 2:3] == expert, info_c[:, 5:6], 0.0
    )
    act_grad = back * gate
    gate_pre, up_pre = gate_up[:, :hidden], gate_up[:, hidden:]
    s = jax.nn.sigmoid(gate_pre)
    gate_grad = act_grad * up_pre * s * (1.0 + gate_pre * (1.0 - s))
    up_grad = act_grad * (gate_pre * s)
    grad = jnp.concatenate([gate_grad, up_grad], axis=1).astype(BF16)
    pick = picker(
        info_r[0:1, :], info_r[1:2, :], info_r[2:3, :], info_r[3:4, :], expert, n_expert, rows
    )
    hid[0] = jnp.dot(pick, grad, preferred_element_type=F32).astype(BF16)
    term = lax.dot_general(grad, w_in, (((1,), (1,)), ((), ())), preferred_element_type=F32)

    @pl.when(x == 0)
    def _():
        acc[...] = term

    @pl.when(x > 0)
    def _():
        acc[...] += term

    @pl.when(x == local_count - 1)
    def _():
        ret[...] = acc[...].astype(BF16)


def local(tokens, out_grad, routes, gates, w_gate, w_up, w_down_t):
    rows, model = tokens.shape
    n_expert = lax.axis_size("expert")
    n_data = lax.axis_size("dp")
    local_count, width, hidden = w_gate.shape
    count = n_data // 4
    any_, vmem = pl.BlockSpec(memory_space=pl.ANY), pl.BlockSpec(memory_space=pltpu.VMEM)
    dma = pltpu.SemaphoreType.DMA

    flat = routes.reshape(-1)
    onehot = (flat[:, None] == jnp.arange(EXPERTS, dtype=jnp.int32)[None, :]).astype(jnp.int32)
    position = jnp.sum((jnp.cumsum(onehot, axis=0) - 1) * onehot, axis=1).reshape(rows, 2)
    info = jnp.stack(
        [
            routes[:, 0].astype(F32), position[:, 0].astype(F32),
            routes[:, 1].astype(F32), position[:, 1].astype(F32),
            gates[:, 0], gates[:, 1], gates[:, 0], gates[:, 1],
        ]
    )
    side = jnp.concatenate([info[:4].astype(BF16), jnp.zeros((INFO - 4, rows), BF16)], axis=0)
    blocks = jnp.concatenate(
        [
            tokens.T.reshape(n_data, width, rows),
            jnp.broadcast_to(side[None], (n_data, INFO, rows)),
        ],
        axis=1,
    )

    def chain_sems(number):
        return [
            dma((number, count)), dma((number, count)), dma((number, count)),
            dma((number, 2 * count)), dma((number, n_data)),
        ]

    shape = jax.ShapeDtypeStruct
    all_g, all_u, all_dn, tx, ox, ix, tt = pl.pallas_call(
        functools.partial(first_kernel, n_expert, n_data),
        out_shape=(
            shape((local_count, model, hidden), BF16),
            shape((local_count, model, hidden), BF16),
            shape((local_count, model, hidden), BF16),
            shape((n_expert, rows, model), BF16),
            shape((n_expert, rows, model), BF16),
            shape((n_expert, 8, rows), F32),
            shape((width + INFO, n_expert * n_data * rows), BF16),
        ),
        in_specs=[vmem] * 7,
        out_specs=[any_] * 7,
        scratch_shapes=[dma((7,))]
        + chain_sems(3)
        + [
            dma((3, n_expert)), dma((3, n_expert)), dma((n_data,)), dma((n_data,)),
            dma((n_expert,)), dma((n_expert,)),
        ],
        compiler_params=pltpu.CompilerParams(collective_id=0, has_side_effects=True),
    )(w_gate, w_up, w_down_t, tokens, out_grad, info, blocks)

    total = n_expert * rows
    slots = n_expert * CAP
    hid, ret = pl.pallas_call(
        functools.partial(compute_kernel, n_expert),
        grid=(local_count,),
        out_shape=(shape((local_count, slots, 2 * hidden), BF16), shape((total, model), BF16)),
        in_specs=[
            pl.BlockSpec((total, model), lambda x: (0, 0)),
            pl.BlockSpec((total, model), lambda x: (0, 0)),
            pl.BlockSpec((n_expert, 8, rows), lambda x: (0, 0, 0)),
            pl.BlockSpec((1, model, hidden), lambda x: (x, 0, 0)),
            pl.BlockSpec((1, model, hidden), lambda x: (x, 0, 0)),
            pl.BlockSpec((1, model, hidden), lambda x: (x, 0, 0)),
        ],
        out_specs=[
            pl.BlockSpec((1, slots, 2 * hidden), lambda x: (x, 0, 0)),
            pl.BlockSpec((total, model), lambda x: (0, 0)),
        ],
        scratch_shapes=[pltpu.VMEM((total, model), F32)],
        compiler_params=pltpu.CompilerParams(vmem_limit_bytes=60 * 1024 * 1024),
    )(tx.reshape(total, model), ox.reshape(total, model), ix, all_g, all_u, all_dn)

    grad_scale = 1.0 / math.sqrt(rows * n_expert * n_data)
    token_grad, grad_gate, grad_up = pl.pallas_call(
        functools.partial(second_kernel, n_expert, n_data),
        out_shape=(
            shape((rows, model), BF16),
            shape((local_count, width, hidden), F32),
            shape((local_count, width, hidden), F32),
        ),
        in_specs=[vmem] * 3,
        out_specs=[vmem] * 3,
        scratch_shapes=[
            pltpu.VMEM((n_data, local_count, slots, 2 * hidden), BF16),
            pltpu.VMEM((n_expert, rows, model), BF16),
            dma,
        ]
        + chain_sems(1)
        + [dma((n_expert,)), dma((n_expert,))],
        compiler_params=pltpu.CompilerParams(
            collective_id=1, has_side_effects=True, vmem_limit_bytes=60 * 1024 * 1024
        ),
    )(hid, ret.reshape(n_expert, rows, model), tt)
    return token_grad, grad_gate * grad_scale, grad_up * grad_scale


def solution(mesh):
    row, split = P(("expert", "dp"), None), P("expert", "dp", None)
    return jax.shard_map(
        local,
        mesh=mesh,
        in_specs=(row, row, row, row, split, split, split),
        out_specs=(row, split, split),
        check_vma=False,
    )
```

```python
import functools
import math

import jax
import jax.numpy as jnp
from jax import lax
from jax.experimental import pallas as pl
from jax.experimental.pallas import tpu as pltpu
from jax.sharding import PartitionSpec as P

EXPERTS = 8
CAP = 40
INFO = 16
F32 = jnp.float32
BF16 = jnp.bfloat16


def remote(src, dst, send, recv, e, d):
    return pltpu.make_async_remote_copy(
        src_ref=src,
        dst_ref=dst,
        send_sem=send,
        recv_sem=recv,
        device_id={"expert": e, "dp": d},
        device_id_type=pl.DeviceIdType.MESH,
    )


def when(cond, fn):
    if cond is None:
        fn()
    else:
        pl.when(cond)(fn)


class Sends:
    def __init__(self):
        self.items = []

    def start(self, cond, make):
        when(cond, lambda: make().start())
        self.items.append((cond, make))

    def finish(self):
        for cond, make in self.items:
            when(cond, lambda make=make: make().wait_send())


def barrier(e, d, n_expert, n_data):
    sem = pltpu.get_barrier_semaphore()
    for j in range(1, n_data):
        pl.semaphore_signal(
            sem,
            inc=1,
            device_id={"expert": e, "dp": lax.rem(d + j, n_data)},
            device_id_type=pl.DeviceIdType.MESH,
        )
    for j in range(1, n_expert):
        pl.semaphore_signal(
            sem,
            inc=1,
            device_id={"expert": lax.rem(e + j, n_expert), "dp": d},
            device_id_type=pl.DeviceIdType.MESH,
        )
    pl.semaphore_wait(sem, n_data - 1 + n_expert - 1)


def both(p, q):
    if p is None:
        return q
    return jnp.logical_and(p, q)


def gather(e, d, n_data, owns, block, sems, sends, hook=None, use=None):
    up_s, down_s, b_s, c_s, recv = sems
    count = n_data // 4
    a, b, c = d // 4, lax.rem(d // 2, 2), lax.rem(d, 2)
    number = len(owns)

    def index(a2, b2, c2):
        return (a2 * 2 + b2) * 2 + c2

    def make(i, src, d2, target, send):
        return remote(src, block(i, d2), send, recv.at[i, d2], e, target)

    def arrive(i, d2):
        remote(block(i, d2), block(i, d2), c_s.at[i, 0], recv.at[i, d2], e, d).wait_recv()

    def pass_on(cond, i, src, a2, up, down, slot):
        d2 = index(a2, b, c)
        if up:
            sends.start(
                both(cond, a < count - 1),
                lambda: make(i, src(), d2, index(a + 1, b, c), up_s.at[i, slot]),
            )
        if down:
            sends.start(
                both(cond, a > 0),
                lambda: make(i, src(), d2, index(a - 1, b, c), down_s.at[i, slot]),
            )
        sends.start(cond, lambda: make(i, src(), d2, index(a, 1 - b, c), b_s.at[i, a2]))
        sends.start(cond, lambda: make(i, src(), d2, index(a, b, 1 - c), c_s.at[i, a2 * 2 + b]))

    def from_b(cond, a2):
        d2 = index(a2, 1 - b, c)
        for i in range(number):
            when(cond, lambda i=i: arrive(i, d2))
            sends.start(
                cond,
                lambda i=i: make(
                    i, block(i, d2), d2, index(a, b, 1 - c), c_s.at[i, a2 * 2 + 1 - b]
                ),
            )

    for step in range(count + 2):
        if step == 0:
            for i in range(number):
                pass_on(None, i, lambda i=i: owns[i], a, True, True, 0)
        elif step < count:
            for i in range(number):
                cond, a2 = a >= step, a - step
                d2 = index(a2, b, c)
                when(cond, lambda i=i, d2=d2: arrive(i, d2))
                pass_on(cond, i, lambda i=i, d2=d2: block(i, d2), a2, True, False, step)
                cond, a2 = a + step < count, a + step
                d2 = index(a2, b, c)
                when(cond, lambda i=i, d2=d2: arrive(i, d2))
                pass_on(cond, i, lambda i=i, d2=d2: block(i, d2), a2, False, True, step)
        if step == 1:
            from_b(None, a)
        elif 1 < step <= count:
            from_b(a >= step - 1, a - step + 1)
            from_b(a + step - 1 < count, a + step - 1)
        if hook is not None:
            hook(step, count)

        def job(j, carry, step=step):
            flip_b, flip_c, way = lax.rem(j // 2, 2), j // 4, lax.rem(j, 2)
            shift = step - flip_b - flip_c
            a2 = a - shift + 2 * shift * way
            d2 = index(a2, b + flip_b * (1 - 2 * b), c + flip_c * (1 - 2 * c))
            far = jnp.logical_or(shift > 0, jnp.logical_and(shift == 0, way == 0))
            valid = jnp.logical_and(far, jnp.logical_and(a2 >= 0, a2 < count))

            @pl.when(jnp.logical_and(valid, flip_c == 1))
            def _():
                for i in range(number):
                    arrive(i, d2)

            if use is not None:
                pl.when(valid)(lambda: use(d2))
            return carry

        lax.fori_loop(0, 8, job, 0)


def first_kernel(
    n_expert, n_data, w_g, w_u, w_dn, tok, og, info, blocks,
    all_g, all_u, all_dn, tx, ox, ix, tt,
    own_sem, up_s, down_s, b_s, c_s, recv, x_s, x_r, t_s, t_r, y_s, y_r,
):
    e, d = lax.axis_index("expert"), lax.axis_index("dp")
    width = w_g.shape[1]
    rows = tok.shape[0]

    def block(i, d2):
        return (all_g, all_u, all_dn)[i].at[:, pl.ds(d2 * width, width), :]

    def columns(e2, d2):
        return tt.at[:, pl.ds(pl.multiple_of((e2 * n_data + d2) * rows, rows), rows)]

    def half(e2):
        return tt.at[:, pl.ds(pl.multiple_of(e2 * n_data * rows, n_data * rows), n_data * rows)]

    own = [
        pltpu.make_async_copy(w_g, block(0, d), own_sem.at[0]),
        pltpu.make_async_copy(w_dn, block(2, d), own_sem.at[1]),
        pltpu.make_async_copy(tok, tx.at[e], own_sem.at[2]),
        pltpu.make_async_copy(og, ox.at[e], own_sem.at[3]),
        pltpu.make_async_copy(info, ix.at[e], own_sem.at[4]),
        pltpu.make_async_copy(blocks.at[d], columns(e, d), own_sem.at[5]),
        pltpu.make_async_copy(w_u, block(1, d), own_sem.at[6]),
    ]
    for copy in own:
        copy.start()
    barrier(e, d, n_expert, n_data)
    sends = Sends()
    triples = ((tok, tx), (og, ox), (info, ix))

    def hook(step, count):
        if step == 0:
            spread()
        if step == max(count - 2, 0):
            relay()

    def spread():
        for j in range(1, n_expert):
            for i, (src, dst) in enumerate(triples):
                sends.start(
                    None,
                    lambda i=i, j=j, src=src, dst=dst: remote(
                        src, dst.at[e], x_s.at[i, j], x_r.at[i, j], lax.rem(e + j, n_expert), d
                    ),
                )
        for j in range(1, n_data):
            sends.start(
                None,
                lambda j=j: remote(
                    blocks.at[lax.rem(d + j, n_data)], columns(e, d), t_s.at[j], t_r.at[j],
                    e, lax.rem(d + j, n_data),
                ),
            )

    def relay():
        own[5].wait()
        for j in range(1, n_data):
            source = lax.rem(d - j + n_data, n_data)
            place = columns(e, source)
            remote(place, place, t_s.at[j], t_r.at[j], e, source).wait_recv()
        for j in range(1, n_expert):
            sends.start(
                None,
                lambda j=j: remote(
                    half(e), half(e), y_s.at[j], y_r.at[j], lax.rem(e + j, n_expert), d
                ),
            )

    gather(e, d, n_data, (w_g, w_u, w_dn), block, (up_s, down_s, b_s, c_s, recv), sends, hook)
    for copy in own[:5] + own[6:]:
        copy.wait()
    for j in range(1, n_expert):
        source = lax.rem(e - j + n_expert, n_expert)
        for i, (src, dst) in enumerate(triples):
            remote(src, dst.at[source], x_s.at[i, j], x_r.at[i, j], source, d).wait_recv()
        remote(half(source), half(source), y_s.at[j], y_r.at[j], source, d).wait_recv()
    sends.finish()


def second_kernel(
    n_expert, n_data, scale, hid, ret, tt, tg, out_g, out_u,
    all_hid, rx, own_sem, up_s, down_s, b_s, c_s, recv, x_s, x_r,
):
    e, d = lax.axis_index("expert"), lax.axis_index("dp")
    local_count, width, hidden = out_g.shape
    rows = tt.shape[1] // (n_expert * n_data)

    def block(i, d2):
        return all_hid.at[d2]

    own = pltpu.make_async_copy(hid, block(0, d), own_sem)
    own.start()
    barrier(e, d, n_expert, n_data)
    sends = Sends()

    def hook(step, count):
        if step > 0:
            return
        for j in range(1, n_expert):
            target = lax.rem(e + j, n_expert)
            sends.start(
                None,
                lambda j=j, target=target: remote(
                    ret.at[target], rx.at[e], x_s.at[j], x_r.at[j], target, d
                ),
            )
        out_g[...] = jnp.zeros_like(out_g)
        out_u[...] = jnp.zeros_like(out_u)
        own.wait()

    def use(d2):
        parts = [
            tt[:, pl.ds(pl.multiple_of((s * n_data + d2) * rows, rows), rows)]
            for s in range(n_expert)
        ]
        both_tt = jnp.concatenate(parts, axis=1)
        tok, info = both_tt[:width], both_tt[width:].astype(F32)
        for x in range(local_count):
            expert = (e * local_count + x).astype(F32)
            pick = picker(info[0:1], info[1:2], info[2:3], info[3:4], expert, n_expert, rows)
            got = lax.dot_general(
                tok, pick, (((1,), (1,)), ((), ())), preferred_element_type=F32
            ).astype(BF16)
            term = jnp.dot(got, all_hid[d2, x], preferred_element_type=F32)
            out_g[x] += term[:, :hidden]
            out_u[x] += term[:, hidden:]

    gather(e, d, n_data, (hid,), block, (up_s, down_s, b_s, c_s, recv), sends, hook, use)
    out_g[...] = out_g[...] * scale
    out_u[...] = out_u[...] * scale
    total = ret[e].astype(F32)
    for j in range(1, n_expert):
        source = lax.rem(e - j + n_expert, n_expert)
        remote(ret.at[source], rx.at[source], x_s.at[j], x_r.at[j], source, d).wait_recv()
        total += rx[source].astype(F32)
    tg[...] = total.astype(BF16)
    sends.finish()


def picker(e0, p0, e1, p1, expert, n_expert, rows):
    shape = (n_expert * CAP, n_expert * rows)
    slot = lax.broadcasted_iota(jnp.int32, shape, 0)
    base = (lax.broadcasted_iota(jnp.int32, (1, shape[1]), 1) // rows) * CAP
    want0 = jnp.where(e0 == expert, p0.astype(jnp.int32) + base, -1)
    want1 = jnp.where(e1 == expert, p1.astype(jnp.int32) + base, -1)
    hit = jnp.logical_or(slot == want0, slot == want1)
    return jnp.where(hit, 1.0, 0.0).astype(BF16)


def compute_kernel(n_expert, tx, ox, ix, w_g, w_u, w_dn, hid, ret, acc):
    x, local_count = pl.program_id(0), pl.num_programs(0)
    hidden = w_dn.shape[2]
    rows = tx.shape[0] // n_expert
    expert = (lax.axis_index("expert") * local_count + x).astype(F32)
    info_r = jnp.concatenate([ix[s] for s in range(n_expert)], axis=1)
    info_c = info_r.T
    w_in = jnp.concatenate([w_g[0], w_u[0]], axis=1)
    gate_up = jnp.dot(tx[...], w_in, preferred_element_type=F32)
    back = jnp.dot(ox[...], w_dn[0], preferred_element_type=F32)
    gate = jnp.where(info_c[:, 0:1] == expert, info_c[:, 4:5], 0.0) + jnp.where(
        info_c[:, 2:3] == expert, info_c[:, 5:6], 0.0
    )
    act_grad = back * gate
    gate_pre, up_pre = gate_up[:, :hidden], gate_up[:, hidden:]
    s = jax.nn.sigmoid(gate_pre)
    gate_grad = act_grad * up_pre * s * (1.0 + gate_pre * (1.0 - s))
    up_grad = act_grad * (gate_pre * s)
    grad = jnp.concatenate([gate_grad, up_grad], axis=1).astype(BF16)
    pick = picker(
        info_r[0:1, :], info_r[1:2, :], info_r[2:3, :], info_r[3:4, :], expert, n_expert, rows
    )
    hid[0] = jnp.dot(pick, grad, preferred_element_type=F32).astype(BF16)
    term = lax.dot_general(grad, w_in, (((1,), (1,)), ((), ())), preferred_element_type=F32)

    @pl.when(x == 0)
    def _():
        acc[...] = term

    @pl.when(x > 0)
    def _():
        acc[...] += term

    @pl.when(x == local_count - 1)
    def _():
        ret[...] = acc[...].astype(BF16)


def local(tokens, out_grad, routes, gates, w_gate, w_up, w_down_t):
    rows, model = tokens.shape
    n_expert = lax.axis_size("expert")
    n_data = lax.axis_size("dp")
    local_count, width, hidden = w_gate.shape
    count = n_data // 4
    any_, vmem = pl.BlockSpec(memory_space=pl.ANY), pl.BlockSpec(memory_space=pltpu.VMEM)
    dma = pltpu.SemaphoreType.DMA

    flat = routes.reshape(-1)
    onehot = (flat[:, None] == jnp.arange(EXPERTS, dtype=jnp.int32)[None, :]).astype(jnp.int32)
    position = jnp.sum((jnp.cumsum(onehot, axis=0) - 1) * onehot, axis=1).reshape(rows, 2)
    info = jnp.stack(
        [
            routes[:, 0].astype(F32), position[:, 0].astype(F32),
            routes[:, 1].astype(F32), position[:, 1].astype(F32),
            gates[:, 0], gates[:, 1], gates[:, 0], gates[:, 1],
        ]
    )
    side = jnp.concatenate([info[:4].astype(BF16), jnp.zeros((INFO - 4, rows), BF16)], axis=0)
    blocks = jnp.concatenate(
        [
            tokens.T.reshape(n_data, width, rows),
            jnp.broadcast_to(side[None], (n_data, INFO, rows)),
        ],
        axis=1,
    )

    def chain_sems(number):
        return [
            dma((number, count)), dma((number, count)), dma((number, count)),
            dma((number, 2 * count)), dma((number, n_data)),
        ]

    shape = jax.ShapeDtypeStruct
    all_g, all_u, all_dn, tx, ox, ix, tt = pl.pallas_call(
        functools.partial(first_kernel, n_expert, n_data),
        out_shape=(
            shape((local_count, model, hidden), BF16),
            shape((local_count, model, hidden), BF16),
            shape((local_count, model, hidden), BF16),
            shape((n_expert, rows, model), BF16),
            shape((n_expert, rows, model), BF16),
            shape((n_expert, 8, rows), F32),
            shape((width + INFO, n_expert * n_data * rows), BF16),
        ),
        in_specs=[vmem] * 7,
        out_specs=[any_] * 7,
        scratch_shapes=[dma((7,))]
        + chain_sems(3)
        + [
            dma((3, n_expert)), dma((3, n_expert)), dma((n_data,)), dma((n_data,)),
            dma((n_expert,)), dma((n_expert,)),
        ],
        compiler_params=pltpu.CompilerParams(collective_id=0, has_side_effects=True),
    )(w_gate, w_up, w_down_t, tokens, out_grad, info, blocks)

    total = n_expert * rows
    slots = n_expert * CAP
    hid, ret = pl.pallas_call(
        functools.partial(compute_kernel, n_expert),
        grid=(local_count,),
        out_shape=(shape((local_count, slots, 2 * hidden), BF16), shape((total, model), BF16)),
        in_specs=[
            pl.BlockSpec((total, model), lambda x: (0, 0)),
            pl.BlockSpec((total, model), lambda x: (0, 0)),
            pl.BlockSpec((n_expert, 8, rows), lambda x: (0, 0, 0)),
            pl.BlockSpec((1, model, hidden), lambda x: (x, 0, 0)),
            pl.BlockSpec((1, model, hidden), lambda x: (x, 0, 0)),
            pl.BlockSpec((1, model, hidden), lambda x: (x, 0, 0)),
        ],
        out_specs=[
            pl.BlockSpec((1, slots, 2 * hidden), lambda x: (x, 0, 0)),
            pl.BlockSpec((total, model), lambda x: (0, 0)),
        ],
        scratch_shapes=[pltpu.VMEM((total, model), F32)],
        compiler_params=pltpu.CompilerParams(vmem_limit_bytes=60 * 1024 * 1024),
    )(tx.reshape(total, model), ox.reshape(total, model), ix, all_g, all_u, all_dn)

    grad_scale = 1.0 / math.sqrt(rows * n_expert * n_data)
    token_grad, grad_gate, grad_up = pl.pallas_call(
        functools.partial(second_kernel, n_expert, n_data, grad_scale),
        out_shape=(
            shape((rows, model), BF16),
            shape((local_count, width, hidden), F32),
            shape((local_count, width, hidden), F32),
        ),
        in_specs=[vmem] * 3,
        out_specs=[vmem] * 3,
        scratch_shapes=[
            pltpu.VMEM((n_data, local_count, slots, 2 * hidden), BF16),
            pltpu.VMEM((n_expert, rows, model), BF16),
            dma,
        ]
        + chain_sems(1)
        + [dma((n_expert,)), dma((n_expert,))],
        compiler_params=pltpu.CompilerParams(
            collective_id=1, has_side_effects=True, vmem_limit_bytes=60 * 1024 * 1024
        ),
    )(hid, ret.reshape(n_expert, rows, model), tt)
    return token_grad, grad_gate, grad_up


def solution(mesh):
    row, split = P(("expert", "dp"), None), P("expert", "dp", None)
    return jax.shard_map(
        local,
        mesh=mesh,
        in_specs=(row, row, row, row, split, split, split),
        out_specs=(row, split, split),
        check_vma=False,
    )
```
